128 devices in a mesh: section: 4 (over x), tensor: 16 (over y, z), dp: 2 (over core).
Axes of the slice: x: 4, y: 4, z: 4, core: 2. Of those that a mesh axis runs over, the one named last changes fastest.
Arguments:
- patches: bfloat16 [1536, 8192], P(('section', 'dp'), 'tensor'), may hold values from -12 to 12
- teacher: bfloat16 [1536, 8192], P(('section', 'dp'), 'tensor'), may hold values from -6 to 6
- critic_pairs: int32 [1536, 2], P(('section', 'dp')), may hold values from 0 to 3, as said below
- left_factors: bfloat16 [4, 4, 64, 128, 128], P('section', None, 'tensor'), may hold values from -0.5 to 0.5
- right_factors: bfloat16 [4, 4, 64, 128, 128], P('section', None, 'tensor'), may hold values from -0.5 to 0.5
- norm_gains: bfloat16 [4, 5, 8192], P('section', None, 'tensor'), may hold values from 0.099609375 to 1.8984375
Outputs:
- d_patches: bfloat16 [1536, 8192], P(('section', 'dp'), 'tensor')
- grad_left: float32 [4, 4, 64, 128, 128], P('section', None, 'tensor')
- grad_right: float32 [4, 4, 64, 128, 128], P('section', None, 'tensor')
The draws below stay inside these ranges and needn't reach their ends.
Inputs may be any that keep to these rules, and one draw needn't show every extreme that they name: `critic_pairs`: each row names two different critics. The rows are cut into aligned blocks, each block being the 192 rows of one index of section+dp. In each block, exactly one third of the rows name the pair of critics 0 and 1. Exactly one sixth of the rows name each of the pairs 0 and 2, 0 and 3, 1 and 2, and 1 and 3. No row names critics 2 and 3 together. So critics 0 and 1 are each named by two thirds of a block's rows, and critics 2 and 3 by one third each. Which rows and which column order are random.
All inputs are finite; a program needn't handle non-finite values.
Results may differ from the reference program's by a relative error of at most 0.012.
Values may be sent and summed in bfloat16 or wider, within the bound.
A program may use at most 64 MiB of HBM per device.

```python
import math
import jax
import jax.numpy as jnp
from jax import lax

NB = 64
BS = 128
D = 8192
CRITICS = 4
LAYERS = 4
TOK_DEV = 192
TOKENS = 1536


def draw_patches(key, part):
    base_key, rough_key = jax.random.split(jax.random.fold_in(key, 21), 2)
    position = jnp.arange(D, dtype=jnp.float32) / D
    roughness = jax.random.uniform(rough_key, (D,), jnp.float32, 0.5, 1.5)
    rising = jnp.exp(jnp.log(3.0) * position)
    values = jax.random.normal(base_key, (TOKENS, D), jnp.float32)
    return jnp.clip(values * roughness[None, :] * rising[None, :], -12.0, 12.0).astype(jnp.bfloat16)


def draw_teacher(key, part):
    noise_key, size_key, sign_key = jax.random.split(jax.random.fold_in(key, 31), 3)
    magnitude = jax.random.uniform(size_key, (TOKENS, 1), jnp.float32, 2.0, 3.5)
    direction = 2.0 * jax.random.randint(sign_key, (TOKENS, 1), 0, 2).astype(jnp.float32) - 1.0
    noise = jnp.clip(jax.random.normal(noise_key, (TOKENS, D), jnp.float32), -2.5, 2.5)
    return jnp.clip(noise + direction * magnitude, -6.0, 6.0).astype(jnp.bfloat16)


def draw_critic_pairs(key, part):
    blocks = TOKENS // TOK_DEV
    block_keys = jax.random.split(jax.random.fold_in(key, 11), blocks)
    rank_order = jax.vmap(lambda block_key: jax.random.permutation(block_key, TOK_DEV))(block_keys).astype(jnp.int32)
    pair_class = rank_order * 6 // TOK_DEV
    first_ids = jnp.array([0, 0, 0, 0, 1, 1], jnp.int32)
    second_ids = jnp.array([1, 1, 2, 3, 2, 3], jnp.int32)
    smaller = first_ids[pair_class]
    larger = second_ids[pair_class]
    swapped = jax.random.randint(jax.random.fold_in(key, 12), (blocks, TOK_DEV), 0, 2)
    column_one = jnp.where(swapped == 1, larger, smaller)
    column_two = jnp.where(swapped == 1, smaller, larger)
    return jnp.stack([column_one, column_two], axis=-1).reshape(TOKENS, 2).astype(jnp.int32)


def block_levels(own_key, dims, cuts, smallest, top_value):
    def one(axis_at, blocks):
        draws = jax.random.uniform(jax.random.fold_in(jax.random.fold_in(own_key, 6), axis_at), (blocks,), jnp.float32, smallest / len(cuts), top_value / len(cuts))
        return jnp.repeat(jnp.exp(draws), dims[axis_at] // blocks).reshape((-1,) + (1,) * (len(dims) - axis_at - 1))

    loudness = one(*cuts[0])
    for cut in cuts[1:]:
        loudness = loudness * one(*cut)
    return loudness


def bell_draw(own_key, shape, deviation, reach, shards=(), held_as=jnp.bfloat16):
    drawn = jax.random.normal(own_key, shape, jnp.float32) * deviation
    if len(shards) > 0:
        drawn = block_levels(own_key, shape, shards, -0.22, 0.18) * drawn
    return jnp.clip(drawn, min=-reach, max=reach).astype(held_as)


def setup_inputs(seed: int = 0) -> dict:
    splits = jax.random.split(jax.random.key(seed), 7)
    patches = draw_patches(jax.random.fold_in(splits[6], 71), 0)
    teacher = draw_teacher(jax.random.fold_in(splits[6], 71), 0)
    critic_pairs = draw_critic_pairs(jax.random.fold_in(splits[6], 71), 0)
    left_factors = bell_draw(splits[3], (CRITICS, LAYERS, NB, BS, BS), BS ** -0.5, 0.5, ((0, 4), (2, 16)))
    right_factors = bell_draw(splits[4], (CRITICS, LAYERS, NB, BS, BS), BS ** -0.5, 0.5, ((0, 4), (2, 16)))
    norm_gains = jnp.clip(1.0 + 0.18 * jax.random.normal(splits[5], (CRITICS, LAYERS + 1, D), jnp.float32), 0.099609375, 1.8984375).astype(jnp.bfloat16)
    return dict(patches=patches, teacher=teacher, critic_pairs=critic_pairs, left_factors=left_factors, right_factors=right_factors, norm_gains=norm_gains)


EPSILON = 1e-06
TANH_SLOPE = 0.7978845608028654
CUBIC_TERM = 0.044715

def gelu_value(values):
    tangent = jnp.tanh(TANH_SLOPE * (values + CUBIC_TERM * values * values * values))
    return 0.5 * values * (1.0 + tangent)

def gelu_slope(values):
    tangent = jnp.tanh(TANH_SLOPE * (values + CUBIC_TERM * values * values * values))
    return 0.5 * (1.0 + tangent) + 0.5 * values * (1.0 - tangent * tangent) * TANH_SLOPE * (1.0 + 3.0 * CUBIC_TERM * values * values)

def norm_forward(residual, gain_row):
    squares = lax.optimization_barrier(jnp.sum(residual * residual, axis=(1, 2)))
    factor = lax.rsqrt(squares / D + EPSILON)
    return (factor, residual * factor[:, None, None] * gain_row.astype(jnp.float32).reshape(1, NB, BS))

def norm_backward(residual, factor, gain_row, grad_normed, carried):
    weighted = grad_normed * gain_row.astype(jnp.float32).reshape(1, NB, BS)
    inners = lax.optimization_barrier(jnp.sum(weighted * residual, axis=(1, 2)))
    return carried + factor[:, None, None] * weighted - residual * (factor ** 3 * inners / D)[:, None, None]

def critic_pass(residual, target, left_blocks, right_blocks, gain_set):
    row_count = residual.shape[0]
    fold_ratio = BS // NB
    stored = []
    for layer_index in range(LAYERS):
        factor, normed = norm_forward(residual, gain_set[layer_index])
        normed = normed.astype(jnp.bfloat16)
        first_out = jnp.einsum('nki,kij->nkj', normed.astype(jnp.float32), left_blocks[layer_index].astype(jnp.float32)).astype(jnp.bfloat16)
        permuted = first_out.reshape(row_count, NB, NB, fold_ratio)
        right_quad = right_blocks[layer_index].reshape(NB, fold_ratio, NB, BS).astype(jnp.float32)
        mixture = jnp.einsum('nkmp,mpkl->nml', permuted.astype(jnp.float32), right_quad)
        stored.append((residual, factor, normed, permuted, mixture, right_quad))
        residual = residual + gelu_value(mixture)
    factor, output = norm_forward(residual, gain_set[LAYERS])
    gradient = norm_backward(residual, factor, gain_set[LAYERS], output - target.astype(jnp.float32), jnp.zeros_like(residual))
    left_list = []
    right_list = []
    for layer_index in range(LAYERS - 1, -1, -1):
        inputs, factor, normed, permuted, mixture, right_quad = stored[layer_index]
        slopes = (gradient * gelu_slope(mixture)).astype(jnp.bfloat16)
        right_grad = jnp.einsum('nkmp,nml->mpkl', permuted.astype(jnp.float32), slopes.astype(jnp.float32)).reshape(NB, BS, BS)
        arrived = jnp.einsum('nml,mpkl->nkmp', slopes.astype(jnp.float32), right_quad).astype(jnp.bfloat16).reshape(row_count, NB, BS)
        left_grad = jnp.einsum('nki,nkj->kij', normed.astype(jnp.float32), arrived.astype(jnp.float32))
        grad_normed = jnp.einsum('nkj,kij->nki', arrived.astype(jnp.float32), left_blocks[layer_index].astype(jnp.float32))
        gradient = norm_backward(inputs, factor, gain_set[layer_index], grad_normed, gradient)
        left_list.insert(0, left_grad)
        right_list.insert(0, right_grad)
    return (gradient.astype(jnp.bfloat16), jnp.stack(left_list), jnp.stack(right_list))

def reference(patches, teacher, critic_pairs, left_factors, right_factors, norm_gains):
    accumulated = jnp.zeros((TOKENS, D), jnp.float32)
    left_all = []
    right_all = []
    for critic in range(CRITICS):
        member_count = TOKENS // 6 * (4 if critic < 2 else 2)
        named_by = jnp.any(critic_pairs == critic, axis=1)
        sort_keys = jnp.where(named_by, 0, 1).astype(jnp.int32)
        row_ids = jnp.argsort(sort_keys, stable=True)[:member_count].astype(jnp.int32)
        residual = patches[row_ids].astype(jnp.float32).reshape(member_count, NB, BS)
        target = teacher[row_ids].reshape(member_count, NB, BS)
        returned, left_grad, right_grad = critic_pass(residual, target, left_factors[critic], right_factors[critic], norm_gains[critic])
        accumulated = accumulated.at[row_ids].add(returned.reshape(member_count, D).astype(jnp.float32))
        left_all.append(left_grad)
        right_all.append(right_grad)
    grad_factor = 1.0 / math.sqrt(2 * TOKENS)
    return ((accumulated * 0.5).astype(jnp.bfloat16), jnp.stack(left_all) * grad_factor, jnp.stack(right_all) * grad_factor)
```

```python
import functools
import math

import jax
import jax.numpy as jnp
from jax import lax
from jax.experimental import pallas as pl
from jax.experimental.pallas import tpu as pltpu
from jax.sharding import PartitionSpec as P

EPSILON = 1e-06
TANH_SLOPE = 0.7978845608028654
CUBIC_TERM = 0.044715
MESH = pl.DeviceIdType.MESH
LANES = 128
CHUNKS = 3
F32 = jnp.float32
BF16 = jnp.bfloat16


def gelu_both(v):
    square = v * v
    tangent = jnp.tanh(TANH_SLOPE * (v + CUBIC_TERM * square * v))
    half = 0.5 + 0.5 * tangent
    slope = half + v * half * (1.0 - tangent) * (TANH_SLOPE + 3.0 * CUBIC_TERM * TANH_SLOPE * square)
    return v * half, slope


def dot(a, b, dims):
    return lax.dot_general(a, b, (dims, ((), ())), preferred_element_type=F32)


NN = ((1,), (0,))
TN = ((0,), (0,))
NT = ((1,), (1,))


def kernel(
    width,
    layers,
    blocks,
    total_tokens,
    patches,
    teacher,
    pairs,
    left,
    right,
    gains_in,
    d_out,
    gl_out,
    gr_out,
    raw_p,
    raw_t,
    raw_i,
    wbuf,
    graw,
    gpad,
    gains,
    perm,
    perm_t,
    hot,
    hbuf,
    hg,
    zn,
    bbuf,
    slope,
    sbuf,
    gbuf,
    tbuf,
    gb16,
    ga16,
    amsg,
    zrecv,
    st_s,
    st_r,
    fst_s,
    fst_r,
    gacc,
    gsend,
    grecv,
    fin,
    d_s,
    d_r,
    m_s,
    m_r,
    t_s,
    t_r,
    f_s,
    f_r,
    w_s,
    w_r,
    n_s,
    n_r,
    raw_s,
    raw_r,
    g_s,
    g_r,
    o_l,
    o_s,
    o_r,
    e_s,
    e_r,
):
    x = lax.axis_index("section")
    t = lax.axis_index("tensor")
    d = lax.axis_index("dp")
    sections = 4
    tok = patches.shape[0]
    bs = LANES
    feat = blocks * bs
    model = feat * width
    all_blocks = blocks * width
    rows = bs // width
    fold = bs // all_blocks
    partner = {"dp": 1 - d}

    barrier = pltpu.get_barrier_semaphore()

    def greet(i, _):
        pl.semaphore_signal(
            barrier, inc=1, device_id={"tensor": lax.rem(t + i, width)}, device_id_type=MESH
        )
        return 0

    lax.fori_loop(1, width, greet, 0)
    pl.semaphore_signal(barrier, inc=1, device_id=partner, device_id_type=MESH)
    for dx in range(1, sections):
        for e in range(2):
            pl.semaphore_signal(
                barrier,
                inc=1,
                device_id={"section": lax.rem(x + dx, sections), "dp": e},
                device_id_type=MESH,
            )

    def column_of(r):
        m = r >> 7
        w = r & (bs - 1)
        q = w >> (all_blocks.bit_length() - 1)
        k = w & (all_blocks - 1)
        return k * rows + m * fold + q

    def fill_perm(i, _):
        base = i * bs
        r = lax.broadcasted_iota(jnp.int32, (bs, feat), 0) + base
        c = lax.broadcasted_iota(jnp.int32, (bs, feat), 1)
        perm[pl.ds(base, bs), :] = jnp.where(column_of(r) == c, 1.0, 0.0).astype(BF16)
        perm_t[pl.ds(base, bs), :] = jnp.where(column_of(c) == r, 1.0, 0.0).astype(BF16)
        return 0

    lax.fori_loop(0, blocks, fill_perm, 0)
    gpad[...] = jnp.zeros_like(gpad)
    gacc[...] = jnp.zeros_like(gacc)

    lower = jnp.where(
        lax.broadcasted_iota(jnp.int32, (tok, tok), 0)
        > lax.broadcasted_iota(jnp.int32, (tok, tok), 1),
        1.0,
        0.0,
    ).astype(BF16)
    lane = lax.broadcasted_iota(jnp.int32, (tok, LANES), 1)

    def one_hot(ids, critic, offset):
        named = jnp.where((ids[:, 0:1] == critic) | (ids[:, 1:2] == critic), 1.0, 0.0)
        named = jnp.broadcast_to(named, (tok, LANES))
        rank = dot(lower, named.astype(BF16), NN)
        at = lane.astype(F32) - offset
        return jnp.where((rank == at) & (named > 0.5), 1.0, 0.0).astype(BF16)

    own_ids = pairs[...]
    hot[0] = one_hot(own_ids, d, 0.0)
    hot[2] = one_hot(own_ids, d + 2, 0.0)
    hbuf[0, 0] = dot(patches[...], hot[0], TN)
    tbuf[0] = dot(teacher[...], hot[0], TN).astype(BF16)

    pl.semaphore_wait(barrier, (width - 1) + 1 + 2 * (sections - 1))

    raws = ((pairs, raw_i), (patches, raw_p), (teacher, raw_t))
    for at, (src, dst) in enumerate(raws):
        pltpu.make_async_remote_copy(
            src_ref=src,
            dst_ref=dst,
            send_sem=raw_s.at[at],
            recv_sem=raw_r.at[at],
            device_id=partner,
            device_id_type=MESH,
        ).start()

    slot_here = x // 2
    runs_here = lax.rem(x, 2) == d
    half = pl.ds(2 * d, 2)
    lane_half = pl.ds(pl.multiple_of(d * (feat // 2), LANES), feat // 2)
    for dx in range(1, sections):
        pltpu.make_async_remote_copy(
            src_ref=gains_in.at[:, lane_half],
            dst_ref=graw.at[slot_here, :, lane_half],
            send_sem=n_s.at[dx - 1],
            recv_sem=n_r.at[slot_here],
            device_id={"section": lax.rem(x + dx, sections), "dp": lax.rem(x, 2)},
            device_id_type=MESH,
        ).start()

    def send_factors(layer, _):
        for f, src in enumerate((left, right)):
            for dx in (2, 1, 3):
                pltpu.make_async_remote_copy(
                    src_ref=src.at[layer, half],
                    dst_ref=wbuf.at[slot_here, layer, f, half],
                    send_sem=w_s,
                    recv_sem=w_r.at[slot_here, layer, f],
                    device_id={"section": lax.rem(x + dx, sections), "dp": lax.rem(x, 2)},
                    device_id_type=MESH,
                ).start()
        return 0

    lax.fori_loop(0, layers, send_factors, 0)

    @pl.when(runs_here)
    def _():
        pltpu.make_async_copy(gains_in, graw.at[slot_here], n_r.at[slot_here]).start()

        def take(layer, _):
            for f, src in enumerate((left, right)):
                pltpu.make_async_copy(
                    src.at[layer], wbuf.at[slot_here, layer, f], w_r.at[slot_here, layer, f]
                ).start()
            return 0

        lax.fori_loop(0, layers, take, 0)

    def await_bytes(ref, sem):
        pltpu.make_async_copy(ref, ref, sem).wait()

    def spread_gains(j):
        await_bytes(graw.at[j], n_r.at[j])
        gpad[j, 0 : layers + 1, :] = graw[j]

        def one(layer, _):
            pick = jnp.where(
                lax.broadcasted_iota(jnp.int32, (16, LANES), 0) == layer, 1.0, 0.0
            ).astype(BF16)
            gains[j, layer] = dot(gpad[j], pick, TN)
            return 0

        lax.fori_loop(0, layers + 1, one, 0)

    spread_gains(0)

    await_bytes(raw_i, raw_r.at[0])
    other_ids = raw_i[...]
    hot[1] = one_hot(other_ids, d, 0.0)
    hot[3] = one_hot(other_ids, d + 2, float(LANES // 2))
    await_bytes(raw_p, raw_r.at[1])
    hbuf[0, 1] = dot(raw_p[...], hot[1], TN)
    hbuf[0, 2] = dot(patches[...], hot[2], TN) + dot(raw_p[...], hot[3], TN)
    spread_gains(1)

    def exchange(step, q):
        def one(i, _):
            peer = lax.rem(t + i, width)
            pltpu.make_async_remote_copy(
                src_ref=st_s.at[step, q],
                dst_ref=st_r.at[step, q, t],
                send_sem=t_s.at[step, q],
                recv_sem=t_r.at[step, q],
                device_id={"tensor": peer},
                device_id_type=MESH,
            ).start()
            pltpu.make_async_remote_copy(
                src_ref=amsg.at[step, q, peer],
                dst_ref=zrecv.at[step, q, t],
                send_sem=m_s.at[step, q],
                recv_sem=m_r.at[step, q],
                device_id={"tensor": peer},
                device_id_type=MESH,
            ).start()
            return 0

        lax.fori_loop(1, width, one, 0)
        pltpu.make_async_copy(st_s.at[step, q], st_r.at[step, q, t], t_r.at[step, q]).start()
        pltpu.make_async_copy(amsg.at[step, q, t], zrecv.at[step, q, t], m_r.at[step, q]).start()

    def fwd_send(layer, q):
        j = q // 2

        @pl.when(q != 1)
        def _():
            await_bytes(wbuf.at[j, layer, 0], w_r.at[j, layer, 0])

        h = hbuf[layer, q]
        st_s[layer, q] = jnp.sum(h * h, axis=0, keepdims=True)
        hg[layer, q] = (h * gains[j, layer]).astype(BF16)
        outs = []
        for k in range(blocks):
            out = dot(wbuf[j, layer, 0, k], hg[layer, q, k * bs : (k + 1) * bs, :], TN)
            outs.append(out.reshape(width, 1, rows, LANES))
        message = jnp.concatenate(outs, axis=1).reshape(width, blocks * rows, LANES)
        amsg[layer, q] = message.astype(BF16)
        exchange(layer, q)

    def fwd_take(layer, q):
        j = q // 2

        @pl.when(q != 1)
        def _():
            await_bytes(wbuf.at[j, layer, 1], w_r.at[j, layer, 1])

        await_bytes(st_r.at[layer, q], t_r.at[layer, q])
        await_bytes(zrecv.at[layer, q], m_r.at[layer, q])
        squares = jnp.sum(st_r[layer, q], axis=0)
        s = lax.rsqrt(squares / model + EPSILON)
        sbuf[layer, q] = s
        zn[layer, q] = dot(perm[...], zrecv[layer, q].reshape(feat, LANES), NN).astype(BF16)
        for m in range(blocks):
            part = slice(m * bs, (m + 1) * bs)
            b = dot(wbuf[j, layer, 1, m], zn[layer, q, part, :], TN) * s
            bbuf[layer, q, part, :] = b
            value, steep = gelu_both(b)
            slope[layer, q, part, :] = steep
            hbuf[layer + 1, q, part, :] = hbuf[layer, q, part, :] + value

    def first(q, _):
        fwd_send(0, q)
        return 0

    lax.fori_loop(0, CHUNKS, first, 0)

    await_bytes(raw_t, raw_r.at[2])
    tbuf[1] = dot(raw_t[...], hot[1], TN).astype(BF16)
    tbuf[2] = (dot(teacher[...], hot[2], TN) + dot(raw_t[...], hot[3], TN)).astype(BF16)

    def forward(i, _):
        layer = i // CHUNKS
        q = lax.rem(i, CHUNKS)
        fwd_take(layer, q)
        fwd_send(layer + 1, q)
        return 0

    lax.fori_loop(0, CHUNKS * (layers - 1), forward, 0)

    def last(q, _):
        fwd_take(layers - 1, q)
        j = q // 2
        h = hbuf[layers, q]
        gh = gains[j, layers] * h
        fst_s[q, 0] = jnp.sum(h * h, axis=0, keepdims=True)
        fst_s[q, 1] = jnp.sum(gh * gh, axis=0, keepdims=True)
        fst_s[q, 2] = jnp.sum(gh * tbuf[q].astype(F32), axis=0, keepdims=True)

        def one(i, _):
            pltpu.make_async_remote_copy(
                src_ref=fst_s.at[q],
                dst_ref=fst_r.at[q, t],
                send_sem=f_s.at[q],
                recv_sem=f_r.at[q],
                device_id={"tensor": lax.rem(t + i, width)},
                device_id_type=MESH,
            ).start()
            return 0

        lax.fori_loop(1, width, one, 0)
        pltpu.make_async_copy(fst_s.at[q], fst_r.at[q, t], f_r.at[q]).start()
        return 0

    lax.fori_loop(0, CHUNKS, last, 0)

    def send_grad(layer, f, j):
        critic = d + 2 * j
        for e in range(2):
            piece = gsend.at[j, layer, f, pl.ds(2 * e, 2)]
            landing = grecv.at[layer, f, x]
            stays = (critic == x) & (d == e)

            @pl.when(stays)
            def _():
                pltpu.make_async_copy(piece, landing, g_r.at[layer, f]).start()

            @pl.when(jnp.logical_not(stays))
            def _():
                pltpu.make_async_remote_copy(
                    src_ref=piece,
                    dst_ref=landing,
                    send_sem=g_s.at[j, layer, f],
                    recv_sem=g_r.at[layer, f],
                    device_id={"section": critic, "dp": e},
                    device_id_type=MESH,
                ).start()

    def factor_grad(layer, f, q, lhs, rhs):
        j = q // 2
        for k in range(blocks):
            part = slice(k * bs, (k + 1) * bs)
            term = dot(lhs[layer, q, part, :], rhs[part, :], NT)
            term = term + jnp.where(q == 1, gacc[f, k], 0.0)
            gacc[f, k] = term
            gsend[j, layer, f, k] = term.astype(BF16)

        @pl.when(q != 0)
        def _():
            send_grad(layer, f, j)

    def bwd_send(layer, q):
        j = q // 2
        step = layers + layer
        gbs = gbuf[q] * slope[layer, q] * sbuf[layer, q]
        st_s[step, q] = jnp.sum(gbs * bbuf[layer, q], axis=0, keepdims=True)
        gb16[...] = gbs.astype(BF16)
        outs = []
        for m in range(blocks):
            out = dot(wbuf[j, layer, 1, m], gb16[m * bs : (m + 1) * bs, :], NN)
            outs.append(out.astype(BF16))
        moved = dot(perm_t[...], jnp.concatenate(outs, axis=0), NN)
        amsg[step, q] = moved.astype(BF16).reshape(width, blocks * rows, LANES)
        exchange(step, q)

    def bwd_take(layer, q):
        j = q // 2
        step = layers + layer
        await_bytes(st_r.at[step, q], t_r.at[step, q])
        await_bytes(zrecv.at[step, q], m_r.at[step, q])
        inner = jnp.sum(st_r[step, q], axis=0)
        coefficient = sbuf[layer, q] * inner / model
        arrived = zrecv[step, q].astype(F32).reshape(width, blocks, rows, LANES)
        for k in range(blocks):
            part = slice(k * bs, (k + 1) * bs)
            ga16[part, :] = arrived[:, k].reshape(bs, LANES).astype(BF16)
            gu = dot(wbuf[j, layer, 0, k], ga16[part, :], NN)
            gbuf[q, part, :] = (
                gbuf[q, part, :]
                + gu * gains[j, layer, part, :]
                - hbuf[layer, q, part, :] * coefficient
            )

    grad_factor = 1.0 / math.sqrt(2 * total_tokens)
    outs = (gl_out, gr_out)

    def finish(layer):
        for f in range(2):
            await_bytes(grecv.at[layer, f], g_r.at[layer, f])
            total = grecv[layer, f, 0].astype(F32)
            for source in range(1, sections):
                total = total + grecv[layer, f, source].astype(F32)
            fin[layer, f] = total * grad_factor
            pltpu.make_async_remote_copy(
                src_ref=fin.at[layer, f],
                dst_ref=outs[f].at[layer, half],
                send_sem=o_s,
                recv_sem=o_r,
                device_id=partner,
                device_id_type=MESH,
            ).start()
            pltpu.make_async_copy(fin.at[layer, f], outs[f].at[layer, half], o_l).start()

    def turn(q, _):
        j = q // 2
        await_bytes(fst_r.at[q], f_r.at[q])
        sums = jnp.sum(fst_r[q], axis=0)
        s = lax.rsqrt(sums[0] / model + EPSILON)
        coefficient = s * s * s * (s * sums[1] - sums[2]) / model
        h = hbuf[layers, q]
        gain = gains[j, layers]
        e = (h * s * gain - tbuf[q].astype(F32)) * gain
        gbuf[q] = s * e - h * coefficient
        bwd_send(layers - 1, q)
        factor_grad(layers - 1, 1, q, zn, gb16)
        return 0

    lax.fori_loop(0, CHUNKS, turn, 0)

    def backward(i, _):
        layer = layers - 1 - i // CHUNKS
        q = lax.rem(i, CHUNKS)
        bwd_take(layer, q)
        bwd_send(layer - 1, q)
        factor_grad(layer, 0, q, hg, ga16)
        factor_grad(layer - 1, 1, q, zn, gb16)

        @pl.when((q == CHUNKS - 1) & (layer < layers - 1))
        def _():
            finish(layer + 1)

        return 0

    lax.fori_loop(0, CHUNKS * (layers - 1), backward, 0)

    def ending(q, _):
        bwd_take(0, q)
        factor_grad(0, 0, q, hg, ga16)
        return 0

    lax.fori_loop(0, CHUNKS, ending, 0)

    lead_own = gbuf[0].astype(BF16)
    lead_other = gbuf[1].astype(BF16)
    trail = gbuf[2].astype(BF16)
    d_s[...] = (dot(hot[1], lead_other, NT) + dot(hot[3], trail, NT)).astype(BF16)
    back = pltpu.make_async_remote_copy(
        src_ref=d_s,
        dst_ref=d_r,
        send_sem=e_s,
        recv_sem=e_r,
        device_id=partner,
        device_id_type=MESH,
    )
    back.start()
    own = dot(hot[0], lead_own, NT) + dot(hot[2], trail, NT)
    finish(1)
    back.wait()
    d_out[...] = ((own + d_r[...].astype(F32)) * 0.5).astype(BF16)
    finish(0)

    def drain(step, _):
        def one(q, _):
            await_bytes(amsg.at[step, q, pl.ds(0, width - 1)], m_s.at[step, q])
            await_bytes(st_r.at[step, q, pl.ds(0, width - 1)], t_s.at[step, q])
            return 0

        return lax.fori_loop(0, CHUNKS, one, 0)

    lax.fori_loop(0, 2 * layers, drain, 0)

    def drain_final(q, _):
        await_bytes(fst_r.at[q, pl.ds(0, width - 1)], f_s.at[q])
        return 0

    lax.fori_loop(0, CHUNKS, drain_final, 0)
    for at, (src, dst) in enumerate(raws):
        await_bytes(src, raw_s.at[at])
    await_bytes(wbuf.at[:, pl.ds(0, 3)], w_s)
    for at in range(sections - 1):
        await_bytes(graw.at[0, :, pl.ds(0, feat // 2)], n_s.at[at])

    def drain_grad(layer, _):
        for j in range(2):
            for f in range(2):
                local = (d + 2 * j) == x

                @pl.when(local)
                def _():
                    await_bytes(gsend.at[j, layer, f, pl.ds(0, 2)], g_s.at[j, layer, f])

                @pl.when(jnp.logical_not(local))
                def _():
                    await_bytes(gsend.at[j, layer, f], g_s.at[j, layer, f])

        return 0

    lax.fori_loop(0, layers, drain_grad, 0)
    await_bytes(fin, o_l)
    await_bytes(fin, o_s)
    await_bytes(fin, o_r)


def shards(width, patches, teacher, critic_pairs, left_factors, right_factors, norm_gains):
    tok, feat = patches.shape
    layers, blocks, bs = left_factors.shape[1:4]
    rows = bs // width
    steps = 2 * layers
    total_tokens = tok * 8
    vmem = pl.BlockSpec(memory_space=pltpu.VMEM)
    anyspace = pl.BlockSpec(memory_space=pl.ANY)
    tile = (feat, LANES)
    message = (steps, CHUNKS, width, blocks * rows, LANES)
    dma = pltpu.SemaphoreType.DMA
    scratch = [
        pltpu.VMEM((tok, feat), BF16),
        pltpu.VMEM((tok, feat), BF16),
        pltpu.VMEM((tok, 2), jnp.int32),
        pltpu.VMEM((2, layers, 2, blocks, bs, bs), BF16),
        pltpu.VMEM((2, layers + 1, feat), BF16),
        pltpu.VMEM((2, 16, feat), BF16),
        pltpu.VMEM((2, layers + 1) + tile, F32),
        pltpu.VMEM((feat, feat), BF16),
        pltpu.VMEM((feat, feat), BF16),
        pltpu.VMEM((4, tok, LANES), BF16),
        pltpu.VMEM((layers + 1, CHUNKS) + tile, F32),
        pltpu.VMEM((layers, CHUNKS) + tile, BF16),
        pltpu.VMEM((layers, CHUNKS) + tile, BF16),
        pltpu.VMEM((layers, CHUNKS) + tile, F32),
        pltpu.VMEM((layers, CHUNKS) + tile, F32),
        pltpu.VMEM((layers, CHUNKS, 1, LANES), F32),
        pltpu.VMEM((CHUNKS,) + tile, F32),
        pltpu.VMEM((CHUNKS,) + tile, BF16),
        pltpu.VMEM(tile, BF16),
        pltpu.VMEM(tile, BF16),
        pltpu.VMEM(message, BF16),
        pltpu.VMEM(message, BF16),
        pltpu.VMEM((steps, CHUNKS, 1, LANES), F32),
        pltpu.VMEM((steps, CHUNKS, width, 1, LANES), F32),
        pltpu.VMEM((CHUNKS, 3, 1, LANES), F32),
        pltpu.VMEM((CHUNKS, width, 3, 1, LANES), F32),
        pltpu.VMEM((2, blocks, bs, bs), F32),
        pltpu.VMEM((2, layers, 2, blocks, bs, bs), BF16),
        pltpu.VMEM((layers, 2, 4, 2, bs, bs), BF16),
        pltpu.VMEM((layers, 2, 2, bs, bs), F32),
        pltpu.VMEM((tok, feat), BF16),
        pltpu.VMEM((tok, feat), BF16),
        dma((steps, CHUNKS)),
        dma((steps, CHUNKS)),
        dma((steps, CHUNKS)),
        dma((steps, CHUNKS)),
        dma((CHUNKS,)),
        dma((CHUNKS,)),
        dma,
        dma((2, layers, 2)),
        dma((3,)),
        dma((2,)),
        dma((3,)),
        dma((3,)),
        dma((2, layers, 2)),
        dma((layers, 2)),
        dma,
        dma,
        dma,
        dma,
        dma,
    ]
    grad_shape = jax.ShapeDtypeStruct((layers, blocks, bs, bs), F32)
    d_patches, grad_left, grad_right = pl.pallas_call(
        functools.partial(kernel, width, layers, blocks, total_tokens),
        out_shape=(jax.ShapeDtypeStruct((tok, feat), BF16), grad_shape, grad_shape),
        in_specs=[vmem] * 6,
        out_specs=(vmem, anyspace, anyspace),
        scratch_shapes=scratch,
        compiler_params=pltpu.CompilerParams(
            collective_id=0, has_side_effects=True, vmem_limit_bytes=60 * 1024 * 1024
        ),
        name="critics",
    )(patches, teacher, critic_pairs, left_factors[0], right_factors[0], norm_gains[0])
    return d_patches, grad_left[None], grad_right[None]


def solution(mesh):
    in_specs = (
        P(("section", "dp"), "tensor"),
        P(("section", "dp"), "tensor"),
        P(("section", "dp"), None),
        P("section", None, "tensor", None, None),
        P("section", None, "tensor", None, None),
        P("section", None, "tensor"),
    )
    out_specs = (
        P(("section", "dp"), "tensor"),
        P("section", None, "tensor", None, None),
        P("section", None, "tensor", None, None),
    )
    body = functools.partial(shards, mesh.shape["tensor"])
    return jax.shard_map(body, mesh=mesh, in_specs=in_specs, out_specs=out_specs, check_vma=False)
```

```python
import functools
import math

import jax
import jax.numpy as jnp
from jax import lax
from jax.experimental import pallas as pl
from jax.experimental.pallas import tpu as pltpu
from jax.sharding import PartitionSpec as P

EPSILON = 1e-06
TANH_SLOPE = 0.7978845608028654
CUBIC_TERM = 0.044715
MESH = pl.DeviceIdType.MESH
LANES = 128
CHUNKS = 3
F32 = jnp.float32
BF16 = jnp.bfloat16


def gelu_both(v):
    square = v * v
    tangent = jnp.tanh(TANH_SLOPE * (v + CUBIC_TERM * square * v))
    half = 0.5 + 0.5 * tangent
    slope = half + v * half * (1.0 - tangent) * (TANH_SLOPE + 3.0 * CUBIC_TERM * TANH_SLOPE * square)
    return v * half, slope


def dot(a, b, dims):
    return lax.dot_general(a, b, (dims, ((), ())), preferred_element_type=F32)


NN = ((1,), (0,))
TN = ((0,), (0,))
NT = ((1,), (1,))


def kernel(
    width,
    layers,
    blocks,
    total_tokens,
    patches,
    teacher,
    pairs,
    left,
    right,
    gains_in,
    d_out,
    gl_out,
    gr_out,
    own_p,
    own_t,
    own_i,
    raw_p,
    raw_t,
    raw_i,
    wbuf,
    graw,
    gpad,
    gains,
    perm,
    perm_t,
    hot,
    hbuf,
    hg,
    zn,
    bbuf,
    slope,
    sbuf,
    gbuf,
    tbuf,
    gb16,
    ga16,
    amsg,
    zrecv,
    st_s,
    st_r,
    fst_s,
    fst_r,
    gsend,
    grecv,
    fin,
    d_s,
    d_r,
    m_s,
    m_r,
    t_s,
    t_r,
    f_s,
    f_r,
    w_s,
    w_r,
    n_s,
    n_r,
    raw_s,
    raw_r,
    g_s,
    g_r,
    o_l,
    o_s,
    o_r,
    e_s,
    e_r,
    in_s,
):
    x = lax.axis_index("section")
    t = lax.axis_index("tensor")
    d = lax.axis_index("dp")
    sections = 4
    tok = patches.shape[0]
    bs = LANES
    feat = blocks * bs
    model = feat * width
    all_blocks = blocks * width
    rows = bs // width
    fold = bs // all_blocks
    partner = {"dp": 1 - d}

    def hops(i):
        return sum(min(part, 4 - part) if part != 3 else 1 for part in (i >> 2, i & 3))

    far_first = sorted(range(1, width), key=lambda i: -hops(i))

    def peer_at(i):
        return jnp.bitwise_xor(t, i)

    loads = [
        pltpu.make_async_copy(src, dst, in_s.at[at])
        for at, (src, dst) in enumerate(((pairs, own_i), (patches, own_p), (teacher, own_t)))
    ]
    for load in loads:
        load.start()

    slot_here = x // 2
    runs_here = lax.rem(x, 2) == d

    barrier = pltpu.get_barrier_semaphore()

    for i in far_first:
        pl.semaphore_signal(barrier, inc=1, device_id={"tensor": peer_at(i)}, device_id_type=MESH)
    pl.semaphore_signal(barrier, inc=1, device_id=partner, device_id_type=MESH)
    for dx in range(1, sections):
        for e in range(2):
            pl.semaphore_signal(
                barrier,
                inc=1,
                device_id={"section": lax.rem(x + dx, sections), "dp": e},
                device_id_type=MESH,
            )

    @pl.when(runs_here)
    def _():
        pltpu.make_async_copy(gains_in, graw.at[slot_here], n_r.at[slot_here]).start()

        def take(layer, _):
            for f, src in enumerate((left, right)):
                pltpu.make_async_copy(
                    src.at[layer], wbuf.at[slot_here, layer, f], w_r.at[slot_here, layer, f]
                ).start()
            return 0

        lax.fori_loop(0, layers, take, 0)

    def column_of(r):
        m = r >> 7
        w = r & (bs - 1)
        q = w >> (all_blocks.bit_length() - 1)
        k = w & (all_blocks - 1)
        return k * rows + m * fold + q

    def fill_perm(i, _):
        base = i * bs
        r = lax.broadcasted_iota(jnp.int32, (bs, feat), 0) + base
        c = lax.broadcasted_iota(jnp.int32, (bs, feat), 1)
        perm[pl.ds(base, bs), :] = jnp.where(column_of(r) == c, 1.0, 0.0).astype(BF16)
        perm_t[pl.ds(base, bs), :] = jnp.where(column_of(c) == r, 1.0, 0.0).astype(BF16)
        return 0

    lax.fori_loop(0, blocks, fill_perm, 0)
    gpad[...] = jnp.zeros_like(gpad)

    row_at = lax.broadcasted_iota(jnp.int32, (tok, tok), 0)
    col_at = lax.broadcasted_iota(jnp.int32, (tok, tok), 1)
    lower = jnp.where(row_at > col_at, 1.0, 0.0).astype(BF16)
    same = jnp.where(row_at == col_at, 1.0, 0.0).astype(BF16)
    lane = lax.broadcasted_iota(jnp.int32, (tok, LANES), 1).astype(F32)

    def one_hot(ids, critic, offset):
        named = jnp.where((ids[0:1, :] == critic) | (ids[1:2, :] == critic), 1.0, 0.0)
        named = jnp.broadcast_to(named, (LANES, tok)).astype(BF16)
        rank = dot(lower, named, NT)
        here = dot(same, named, NT)
        return jnp.where((rank == lane - offset) & (here > 0.5), 1.0, 0.0).astype(BF16)

    loads[0].wait()
    own_ids = own_i[...]
    hot[0] = one_hot(own_ids, d, 0.0)
    hot[2] = one_hot(own_ids, d + 2, 0.0)
    loads[1].wait()
    hbuf[0, 0] = dot(own_p[...], hot[0], TN)
    hbuf[0, 2] = dot(own_p[...], hot[2], TN)

    pl.semaphore_wait(barrier, (width - 1) + 1 + 2 * (sections - 1))

    raws = ((pairs, raw_i), (patches, raw_p), (teacher, raw_t))

    def send_raw(at):
        pltpu.make_async_remote_copy(
            src_ref=raws[at][0],
            dst_ref=raws[at][1],
            send_sem=raw_s.at[at],
            recv_sem=raw_r.at[at],
            device_id=partner,
            device_id_type=MESH,
        ).start()

    send_raw(0)
    send_raw(1)

    half = pl.ds(2 * d, 2)
    lane_half = pl.ds(pl.multiple_of(d * (feat // 2), LANES), feat // 2)
    for dx in (2, 1, 3):
        pltpu.make_async_remote_copy(
            src_ref=gains_in.at[:, lane_half],
            dst_ref=graw.at[slot_here, :, lane_half],
            send_sem=n_s.at[dx - 1],
            recv_sem=n_r.at[slot_here],
            device_id={"section": lax.rem(x + dx, sections), "dp": lax.rem(x, 2)},
            device_id_type=MESH,
        ).start()

    def send_factors(layer, _):
        for f, src in enumerate((left, right)):
            for dx in (2, 1, 3):
                pltpu.make_async_remote_copy(
                    src_ref=src.at[layer, half],
                    dst_ref=wbuf.at[slot_here, layer, f, half],
                    send_sem=w_s,
                    recv_sem=w_r.at[slot_here, layer, f],
                    device_id={"section": lax.rem(x + dx, sections), "dp": lax.rem(x, 2)},
                    device_id_type=MESH,
                ).start()
        return 0

    lax.fori_loop(0, layers, send_factors, 0)
    send_raw(2)

    def await_bytes(ref, sem):
        pltpu.make_async_copy(ref, ref, sem).wait()

    def spread_gains(j, layer):
        pick = jnp.where(
            lax.broadcasted_iota(jnp.int32, (16, LANES), 0) == layer, 1.0, 0.0
        ).astype(BF16)
        gains[j, layer] = dot(gpad[j], pick, TN)

    def first_gain(j):
        await_bytes(graw.at[j], n_r.at[j])
        gpad[j, 0 : layers + 1, :] = graw[j]
        spread_gains(j, 0)

    await_bytes(raw_i, raw_r.at[0])
    other_ids = raw_i[...]
    hot[1] = one_hot(other_ids, d, 0.0)
    hot[3] = one_hot(other_ids, d + 2, float(LANES // 2))
    await_bytes(raw_p, raw_r.at[1])
    hbuf[0, 1] = dot(raw_p[...], hot[1], TN)
    hbuf[0, 2] = hbuf[0, 2] + dot(raw_p[...], hot[3], TN)
    first_gain(0)
    first_gain(1)

    def exchange(step, q):
        for i in far_first:
            peer = peer_at(i)
            pltpu.make_async_remote_copy(
                src_ref=st_s.at[step, q],
                dst_ref=st_r.at[step, q, t],
                send_sem=t_s.at[step, q],
                recv_sem=t_r.at[step, q],
                device_id={"tensor": peer},
                device_id_type=MESH,
            ).start()
            pltpu.make_async_remote_copy(
                src_ref=amsg.at[step, q, peer],
                dst_ref=zrecv.at[step, q, t],
                send_sem=m_s.at[step, q],
                recv_sem=m_r.at[step, q],
                device_id={"tensor": peer},
                device_id_type=MESH,
            ).start()
        pltpu.make_async_copy(st_s.at[step, q], st_r.at[step, q, t], t_r.at[step, q]).start()
        pltpu.make_async_copy(amsg.at[step, q, t], zrecv.at[step, q, t], m_r.at[step, q]).start()

    def fwd_send(layer, q):
        j = q // 2

        @pl.when(q != 1)
        def _():
            await_bytes(wbuf.at[j, layer, 0], w_r.at[j, layer, 0])

        h = hbuf[layer, q]
        st_s[layer, q] = jnp.sum(h * h, axis=0, keepdims=True)
        hg[layer, q] = (h * gains[j, layer]).astype(BF16)
        outs = []
        for k in range(blocks):
            out = dot(wbuf[j, layer, 0, k], hg[layer, q, k * bs : (k + 1) * bs, :], TN)
            outs.append(out.reshape(width, 1, rows, LANES))
        message = jnp.concatenate(outs, axis=1).reshape(width, blocks * rows, LANES)
        amsg[layer, q] = message.astype(BF16)
        exchange(layer, q)

    def fwd_take(layer, q):
        j = q // 2

        @pl.when(q != 1)
        def _():
            await_bytes(wbuf.at[j, layer, 1], w_r.at[j, layer, 1])

        await_bytes(st_r.at[layer, q], t_r.at[layer, q])
        await_bytes(zrecv.at[layer, q], m_r.at[layer, q])
        squares = jnp.sum(st_r[layer, q], axis=0)
        s = lax.rsqrt(squares / model + EPSILON)
        sbuf[layer, q] = s
        zn[layer, q] = dot(perm[...], zrecv[layer, q].reshape(feat, LANES), NN).astype(BF16)
        for m in range(blocks):
            part = slice(m * bs, (m + 1) * bs)
            b = dot(wbuf[j, layer, 1, m], zn[layer, q, part, :], TN) * s
            bbuf[layer, q, part, :] = b
            value, steep = gelu_both(b)
            slope[layer, q, part, :] = steep
            hbuf[layer + 1, q, part, :] = hbuf[layer, q, part, :] + value

    def first(q, _):
        fwd_send(0, q)
        return 0

    lax.fori_loop(0, CHUNKS, first, 0)

    def more_gains(layer, _):
        spread_gains(0, layer)
        spread_gains(1, layer)
        return 0

    lax.fori_loop(1, layers + 1, more_gains, 0)
    loads[2].wait()
    await_bytes(raw_t, raw_r.at[2])
    tbuf[0] = dot(own_t[...], hot[0], TN).astype(BF16)
    tbuf[1] = dot(raw_t[...], hot[1], TN).astype(BF16)
    tbuf[2] = (dot(own_t[...], hot[2], TN) + dot(raw_t[...], hot[3], TN)).astype(BF16)

    def forward(i, _):
        layer = i // CHUNKS
        q = lax.rem(i, CHUNKS)
        fwd_take(layer, q)
        fwd_send(layer + 1, q)
        return 0

    lax.fori_loop(0, CHUNKS * (layers - 1), forward, 0)

    def last(q, _):
        fwd_take(layers - 1, q)
        j = q // 2
        h = hbuf[layers, q]
        gh = gains[j, layers] * h
        fst_s[q, 0] = jnp.sum(h * h, axis=0, keepdims=True)
        fst_s[q, 1] = jnp.sum(gh * gh, axis=0, keepdims=True)
        fst_s[q, 2] = jnp.sum(gh * tbuf[q].astype(F32), axis=0, keepdims=True)

        for i in far_first:
            pltpu.make_async_remote_copy(
                src_ref=fst_s.at[q],
                dst_ref=fst_r.at[q, t],
                send_sem=f_s.at[q],
                recv_sem=f_r.at[q],
                device_id={"tensor": peer_at(i)},
                device_id_type=MESH,
            ).start()
        pltpu.make_async_copy(fst_s.at[q], fst_r.at[q, t], f_r.at[q]).start()
        return 0

    lax.fori_loop(0, CHUNKS, last, 0)

    def send_grad(layer, f, j):
        critic = d + 2 * j
        for e in range(2):
            piece = gsend.at[j, layer, f, pl.ds(2 * e, 2)]
            landing = grecv.at[layer, f, x]
            stays = (critic == x) & (d == e)

            @pl.when(stays)
            def _():
                pltpu.make_async_copy(piece, landing, g_r.at[layer, f]).start()

            @pl.when(jnp.logical_not(stays))
            def _():
                pltpu.make_async_remote_copy(
                    src_ref=piece,
                    dst_ref=landing,
                    send_sem=g_s.at[j, layer, f],
                    recv_sem=g_r.at[layer, f],
                    device_id={"section": critic, "dp": e},
                    device_id_type=MESH,
                ).start()

    def factor_grad(layer, f, q, lhs, rhs):
        @pl.when(q == 1)
        def _():
            for k in range(blocks):
                part = slice(k * bs, (k + 1) * bs)
                acts = jnp.concatenate((lhs[layer, 0, part, :], lhs[layer, 1, part, :]), axis=1)
                backs = jnp.concatenate((rhs[0, part, :], rhs[1, part, :]), axis=1)
                gsend[0, layer, f, k] = dot(acts, backs, NT).astype(BF16)
            send_grad(layer, f, 0)

        @pl.when(q == 2)
        def _():
            for k in range(blocks):
                part = slice(k * bs, (k + 1) * bs)
                gsend[1, layer, f, k] = dot(lhs[layer, 2, part, :], rhs[2, part, :], NT).astype(BF16)
            send_grad(layer, f, 1)

    def bwd_send(layer, q):
        j = q // 2
        step = layers + layer
        gbs = gbuf[q] * slope[layer, q] * sbuf[layer, q]
        st_s[step, q] = jnp.sum(gbs * bbuf[layer, q], axis=0, keepdims=True)
        gb16[q] = gbs.astype(BF16)
        outs = []
        for m in range(blocks):
            out = dot(wbuf[j, layer, 1, m], gb16[q, m * bs : (m + 1) * bs, :], NN)
            outs.append(out.astype(BF16))
        moved = dot(perm_t[...], jnp.concatenate(outs, axis=0), NN)
        amsg[step, q] = moved.astype(BF16).reshape(width, blocks * rows, LANES)
        exchange(step, q)

    def bwd_take(layer, q):
        j = q // 2
        step = layers + layer
        await_bytes(st_r.at[step, q], t_r.at[step, q])
        await_bytes(zrecv.at[step, q], m_r.at[step, q])
        inner = jnp.sum(st_r[step, q], axis=0)
        coefficient = sbuf[layer, q] * inner / model
        arrived = zrecv[step, q].astype(F32).reshape(width, blocks, rows, LANES)
        for k in range(blocks):
            part = slice(k * bs, (k + 1) * bs)
            ga16[q, part, :] = arrived[:, k].reshape(bs, LANES).astype(BF16)
            gu = dot(wbuf[j, layer, 0, k], ga16[q, part, :], NN)
            gbuf[q, part, :] = (
                gbuf[q, part, :]
                + gu * gains[j, layer, part, :]
                - hbuf[layer, q, part, :] * coefficient
            )

    grad_factor = 1.0 / math.sqrt(2 * total_tokens)
    outs = (gl_out, gr_out)

    def finish(layer):
        for f in range(2):
            await_bytes(grecv.at[layer, f], g_r.at[layer, f])
            total = grecv[layer, f, 0].astype(F32)
            for source in range(1, sections):
                total = total + grecv[layer, f, source].astype(F32)
            fin[layer, f] = total * grad_factor
            pltpu.make_async_remote_copy(
                src_ref=fin.at[layer, f],
                dst_ref=outs[f].at[layer, half],
                send_sem=o_s,
                recv_sem=o_r,
                device_id=partner,
                device_id_type=MESH,
            ).start()
            pltpu.make_async_copy(fin.at[layer, f], outs[f].at[layer, half], o_l).start()

    def turn(q, _):
        j = q // 2
        await_bytes(fst_r.at[q], f_r.at[q])
        sums = jnp.sum(fst_r[q], axis=0)
        s = lax.rsqrt(sums[0] / model + EPSILON)
        coefficient = s * s * s * (s * sums[1] - sums[2]) / model
        h = hbuf[layers, q]
        gain = gains[j, layers]
        e = (h * s * gain - tbuf[q].astype(F32)) * gain
        gbuf[q] = s * e - h * coefficient
        bwd_send(layers - 1, q)
        factor_grad(layers - 1, 1, q, zn, gb16)
        return 0

    lax.fori_loop(0, CHUNKS, turn, 0)

    def backward(i, _):
        layer = layers - 1 - i // CHUNKS
        q = lax.rem(i, CHUNKS)
        bwd_take(layer, q)
        bwd_send(layer - 1, q)
        factor_grad(layer, 0, q, hg, ga16)
        factor_grad(layer - 1, 1, q, zn, gb16)

        @pl.when((q == CHUNKS - 1) & (layer == 1))
        def _():
            finish(3)

        return 0

    lax.fori_loop(0, CHUNKS * (layers - 1), backward, 0)

    def ending(q, _):
        bwd_take(0, q)
        factor_grad(0, 0, q, hg, ga16)

        @pl.when(q == 1)
        def _():
            finish(2)

        return 0

    lax.fori_loop(0, CHUNKS, ending, 0)

    lead_own = gbuf[0].astype(BF16)
    lead_other = gbuf[1].astype(BF16)
    trail = gbuf[2].astype(BF16)
    d_s[...] = (dot(hot[1], lead_other, NT) + dot(hot[3], trail, NT)).astype(BF16)
    back = pltpu.make_async_remote_copy(
        src_ref=d_s,
        dst_ref=d_r,
        send_sem=e_s,
        recv_sem=e_r,
        device_id=partner,
        device_id_type=MESH,
    )
    back.start()
    own = dot(hot[0], lead_own, NT) + dot(hot[2], trail, NT)
    finish(1)
    back.wait()
    d_out[...] = ((own + d_r[...].astype(F32)) * 0.5).astype(BF16)
    finish(0)

    def drain(step, _):
        def one(q, _):
            await_bytes(amsg.at[step, q, pl.ds(0, width - 1)], m_s.at[step, q])
            await_bytes(st_r.at[step, q, pl.ds(0, width - 1)], t_s.at[step, q])
            return 0

        return lax.fori_loop(0, CHUNKS, one, 0)

    lax.fori_loop(0, 2 * layers, drain, 0)

    def drain_final(q, _):
        await_bytes(fst_r.at[q, pl.ds(0, width - 1)], f_s.at[q])
        return 0

    lax.fori_loop(0, CHUNKS, drain_final, 0)
    for at, (src, dst) in enumerate(raws):
        await_bytes(dst, raw_s.at[at])
    await_bytes(wbuf.at[:, pl.ds(0, 3)], w_s)
    for at in range(sections - 1):
        await_bytes(graw.at[0, :, pl.ds(0, feat // 2)], n_s.at[at])

    def drain_grad(layer, _):
        for j in range(2):
            for f in range(2):
                local = (d + 2 * j) == x

                @pl.when(local)
                def _():
                    await_bytes(gsend.at[j, layer, f, pl.ds(0, 2)], g_s.at[j, layer, f])

                @pl.when(jnp.logical_not(local))
                def _():
                    await_bytes(gsend.at[j, layer, f], g_s.at[j, layer, f])

        return 0

    lax.fori_loop(0, layers, drain_grad, 0)
    await_bytes(fin, o_l)
    await_bytes(fin, o_s)
    await_bytes(fin, o_r)


def publish_kernel(d_in, gl_in, gr_in, d_out, gl_out, gr_out, d_v, g_v, in_s, out_s):
    layers = gl_in.shape[0]
    moves = [(d_in, d_v, d_out)]
    for f, (src, dst) in enumerate(((gl_in, gl_out), (gr_in, gr_out))):
        for layer in range(layers):
            moves.append((src.at[layer], g_v.at[f, layer], dst.at[layer]))
    takes = [
        pltpu.make_async_copy(src, mid, in_s.at[at]) for at, (src, mid, _) in enumerate(moves)
    ]
    gives = [
        pltpu.make_async_copy(mid, dst, out_s.at[at]) for at, (_, mid, dst) in enumerate(moves)
    ]
    for take in takes:
        take.start()
    for take, give in zip(takes, gives):
        take.wait()
        give.start()
    for give in gives:
        give.wait()


def publish(d_patches, grad_left, grad_right):
    anyspace = pl.BlockSpec(memory_space=pl.ANY)
    arrays = (d_patches, grad_left, grad_right)
    count = 1 + 2 * grad_left.shape[0]
    return pl.pallas_call(
        publish_kernel,
        out_shape=tuple(jax.ShapeDtypeStruct(a.shape, a.dtype) for a in arrays),
        in_specs=[anyspace] * 3,
        out_specs=(anyspace,) * 3,
        scratch_shapes=[
            pltpu.VMEM(d_patches.shape, d_patches.dtype),
            pltpu.VMEM((2,) + grad_left.shape, grad_left.dtype),
            pltpu.SemaphoreType.DMA((count,)),
            pltpu.SemaphoreType.DMA((count,)),
        ],
        compiler_params=pltpu.CompilerParams(vmem_limit_bytes=60 * 1024 * 1024),
        name="publish",
    )(*arrays)


def shards(width, patches, teacher, critic_pairs, left_factors, right_factors, norm_gains):
    tok, feat = patches.shape
    layers, blocks, bs = left_factors.shape[1:4]
    rows = bs // width
    steps = 2 * layers
    total_tokens = tok * 8
    vmem = pl.BlockSpec(memory_space=pltpu.VMEM)
    anyspace = pl.BlockSpec(memory_space=pl.ANY)
    tile = (feat, LANES)
    message = (steps, CHUNKS, width, blocks * rows, LANES)
    dma = pltpu.SemaphoreType.DMA
    scratch = [
        pltpu.VMEM((tok, feat), BF16),
        pltpu.VMEM((tok, feat), BF16),
        pltpu.VMEM((2, tok), jnp.int32),
        pltpu.VMEM((tok, feat), BF16),
        pltpu.VMEM((tok, feat), BF16),
        pltpu.VMEM((2, tok), jnp.int32),
        pltpu.VMEM((2, layers, 2, blocks, bs, bs), BF16),
        pltpu.VMEM((2, layers + 1, feat), BF16),
        pltpu.VMEM((2, 16, feat), BF16),
        pltpu.VMEM((2, layers + 1) + tile, F32),
        pltpu.VMEM((feat, feat), BF16),
        pltpu.VMEM((feat, feat), BF16),
        pltpu.VMEM((4, tok, LANES), BF16),
        pltpu.VMEM((layers + 1, CHUNKS) + tile, F32),
        pltpu.VMEM((layers, CHUNKS) + tile, BF16),
        pltpu.VMEM((layers, CHUNKS) + tile, BF16),
        pltpu.VMEM((layers, CHUNKS) + tile, F32),
        pltpu.VMEM((layers, CHUNKS) + tile, F32),
        pltpu.VMEM((layers, CHUNKS, 1, LANES), F32),
        pltpu.VMEM((CHUNKS,) + tile, F32),
        pltpu.VMEM((CHUNKS,) + tile, BF16),
        pltpu.VMEM((CHUNKS,) + tile, BF16),
        pltpu.VMEM((CHUNKS,) + tile, BF16),
        pltpu.VMEM(message, BF16),
        pltpu.VMEM(message, BF16),
        pltpu.VMEM((steps, CHUNKS, 1, LANES), F32),
        pltpu.VMEM((steps, CHUNKS, width, 1, LANES), F32),
        pltpu.VMEM((CHUNKS, 3, 1, LANES), F32),
        pltpu.VMEM((CHUNKS, width, 3, 1, LANES), F32),
        pltpu.VMEM((2, layers, 2, blocks, bs, bs), BF16),
        pltpu.VMEM((layers, 2, 4, 2, bs, bs), BF16),
        pltpu.VMEM((layers, 2, 2, bs, bs), F32),
        pltpu.VMEM((tok, feat), BF16),
        pltpu.VMEM((tok, feat), BF16),
        dma((steps, CHUNKS)),
        dma((steps, CHUNKS)),
        dma((steps, CHUNKS)),
        dma((steps, CHUNKS)),
        dma((CHUNKS,)),
        dma((CHUNKS,)),
        dma,
        dma((2, layers, 2)),
        dma((3,)),
        dma((2,)),
        dma((3,)),
        dma((3,)),
        dma((2, layers, 2)),
        dma((layers, 2)),
        dma,
        dma,
        dma,
        dma,
        dma,
        dma((3,)),
    ]
    grad_shape = jax.ShapeDtypeStruct((layers, blocks, bs, bs), F32)
    d_patches, grad_left, grad_right = pl.pallas_call(
        functools.partial(kernel, width, layers, blocks, total_tokens),
        out_shape=(jax.ShapeDtypeStruct((tok, feat), BF16), grad_shape, grad_shape),
        in_specs=[anyspace] * 6,
        out_specs=(vmem, anyspace, anyspace),
        scratch_shapes=scratch,
        compiler_params=pltpu.CompilerParams(
            collective_id=0, has_side_effects=True, vmem_limit_bytes=60 * 1024 * 1024
        ),
        name="critics",
    )(patches, teacher, critic_pairs.T, left_factors[0], right_factors[0], norm_gains[0])
    d_patches, grad_left, grad_right = publish(d_patches, grad_left, grad_right)
    return d_patches, grad_left[None], grad_right[None]


def solution(mesh):
    in_specs = (
        P(("section", "dp"), "tensor"),
        P(("section", "dp"), "tensor"),
        P(("section", "dp"), None),
        P("section", None, "tensor", None, None),
        P("section", None, "tensor", None, None),
        P("section", None, "tensor"),
    )
    out_specs = (
        P(("section", "dp"), "tensor"),
        P("section", None, "tensor", None, None),
        P("section", None, "tensor", None, None),
    )
    body = functools.partial(shards, mesh.shape["tensor"])
    return jax.shard_map(body, mesh=mesh, in_specs=in_specs, out_specs=out_specs, check_vma=False)
```

```python
import functools
import math

import jax
import jax.numpy as jnp
from jax import lax
from jax.experimental import pallas as pl
from jax.experimental.pallas import tpu as pltpu
from jax.sharding import PartitionSpec as P

EPSILON = 1e-06
TANH_SLOPE = 0.7978845608028654
CUBIC_TERM = 0.044715
MESH = pl.DeviceIdType.MESH
LANES = 128
CHUNKS = 3
F32 = jnp.float32
BF16 = jnp.bfloat16


def gelu_both(v):
    square = v * v
    tangent = jnp.tanh(TANH_SLOPE * (v + CUBIC_TERM * square * v))
    half = 0.5 + 0.5 * tangent
    slope = half + v * half * (1.0 - tangent) * (TANH_SLOPE + 3.0 * CUBIC_TERM * TANH_SLOPE * square)
    return v * half, slope


def dot(a, b, dims):
    return lax.dot_general(a, b, (dims, ((), ())), preferred_element_type=F32)


NN = ((1,), (0,))
TN = ((0,), (0,))
NT = ((1,), (1,))


def kernel(
    width,
    layers,
    blocks,
    total_tokens,
    patches,
    teacher,
    pairs,
    left,
    right,
    gains_in,
    d_out,
    gl_out,
    gr_out,
    own_p,
    own_t,
    own_i,
    raw_p,
    raw_t,
    raw_i,
    wbuf,
    graw,
    gpad,
    gains,
    perm,
    perm_t,
    rp,
    rpt,
    hot,
    hbuf,
    hg,
    zn,
    bbuf,
    slope,
    sbuf,
    gbuf,
    tbuf,
    gb16,
    ga16,
    amsg,
    zrecv,
    st_s,
    st_r,
    fst_s,
    fst_r,
    gsend,
    grecv,
    fin,
    d_s,
    d_r,
    m_s,
    m_r,
    t_s,
    t_r,
    f_s,
    f_r,
    w_s,
    w_r,
    n_s,
    n_r,
    raw_s,
    raw_r,
    g_s,
    g_r,
    o_l,
    o_s,
    o_r,
    e_s,
    e_r,
    in_s,
):
    x = lax.axis_index("section")
    t = lax.axis_index("tensor")
    d = lax.axis_index("dp")
    sections = 4
    tok = patches.shape[0]
    bs = LANES
    feat = blocks * bs
    model = feat * width
    all_blocks = blocks * width
    rows = bs // width
    fold = bs // all_blocks
    partner = {"dp": 1 - d}

    def hops(i):
        return sum(min(part, 4 - part) if part != 3 else 1 for part in (i >> 2, i & 3))

    far_first = sorted(range(1, width), key=lambda i: -hops(i))

    def peer_at(i):
        return jnp.bitwise_xor(t, i)

    loads = [
        pltpu.make_async_copy(src, dst, in_s.at[at])
        for at, (src, dst) in enumerate(((pairs, own_i), (patches, own_p), (teacher, own_t)))
    ]
    for load in loads:
        load.start()

    slot_here = x // 2
    runs_here = lax.rem(x, 2) == d

    barrier = pltpu.get_barrier_semaphore()

    for i in far_first:
        pl.semaphore_signal(barrier, inc=1, device_id={"tensor": peer_at(i)}, device_id_type=MESH)
    pl.semaphore_signal(barrier, inc=1, device_id=partner, device_id_type=MESH)
    for dx in range(1, sections):
        for e in range(2):
            pl.semaphore_signal(
                barrier,
                inc=1,
                device_id={"section": lax.rem(x + dx, sections), "dp": e},
                device_id_type=MESH,
            )

    @pl.when(runs_here)
    def _():
        pltpu.make_async_copy(gains_in, graw.at[slot_here], n_r.at[slot_here]).start()

        def take(layer, _):
            for f, src in enumerate((left, right)):
                pltpu.make_async_copy(
                    src.at[layer], wbuf.at[slot_here, layer, f], w_r.at[slot_here, layer, f]
                ).start()
            return 0

        lax.fori_loop(0, layers, take, 0)

    def column_of(r):
        m = r >> 7
        w = r & (bs - 1)
        q = w >> (all_blocks.bit_length() - 1)
        k = w & (all_blocks - 1)
        return k * rows + m * fold + q

    def fill_perm(i, _):
        base = i * bs
        r = lax.broadcasted_iota(jnp.int32, (bs, feat), 0) + base
        c = lax.broadcasted_iota(jnp.int32, (bs, feat), 1)
        perm[pl.ds(base, bs), :] = jnp.where(column_of(r) == c, 1.0, 0.0).astype(BF16)
        perm_t[pl.ds(base, bs), :] = jnp.where(column_of(c) == r, 1.0, 0.0).astype(BF16)
        return 0

    lax.fori_loop(0, blocks, fill_perm, 0)
    gpad[...] = jnp.zeros_like(gpad)

    row_at = lax.broadcasted_iota(jnp.int32, (tok, tok), 0)
    col_at = lax.broadcasted_iota(jnp.int32, (tok, tok), 1)
    lower = jnp.where(row_at > col_at, 1.0, 0.0).astype(BF16)
    same = jnp.where(row_at == col_at, 1.0, 0.0).astype(BF16)
    lane = lax.broadcasted_iota(jnp.int32, (tok, LANES), 1).astype(F32)

    def one_hot(ids, critic, offset):
        named = jnp.where((ids[0:1, :] == critic) | (ids[1:2, :] == critic), 1.0, 0.0)
        named = jnp.broadcast_to(named, (LANES, tok)).astype(BF16)
        rank = dot(lower, named, NT)
        here = dot(same, named, NT)
        return jnp.where((rank == lane - offset) & (here > 0.5), 1.0, 0.0).astype(BF16)

    loads[0].wait()
    own_ids = own_i[...]
    hot[0] = one_hot(own_ids, d, 0.0)
    hot[2] = one_hot(own_ids, d + 2, 0.0)
    loads[1].wait()
    hbuf[0, 0] = dot(own_p[...], hot[0], TN)
    hbuf[0, 2] = dot(own_p[...], hot[2], TN)

    pl.semaphore_wait(barrier, (width - 1) + 1 + 2 * (sections - 1))

    raws = ((pairs, raw_i), (patches, raw_p), (teacher, raw_t))

    def send_raw(at):
        pltpu.make_async_remote_copy(
            src_ref=raws[at][0],
            dst_ref=raws[at][1],
            send_sem=raw_s.at[at],
            recv_sem=raw_r.at[at],
            device_id=partner,
            device_id_type=MESH,
        ).start()

    send_raw(0)
    send_raw(1)

    half = pl.ds(2 * d, 2)
    lane_half = pl.ds(pl.multiple_of(d * (feat // 2), LANES), feat // 2)
    for dx in (2, 1, 3):
        pltpu.make_async_remote_copy(
            src_ref=gains_in.at[:, lane_half],
            dst_ref=graw.at[slot_here, :, lane_half],
            send_sem=n_s.at[dx - 1],
            recv_sem=n_r.at[slot_here],
            device_id={"section": lax.rem(x + dx, sections), "dp": lax.rem(x, 2)},
            device_id_type=MESH,
        ).start()

    def send_factors(layer, _):
        for f, src in enumerate((left, right)):
            for dx in (2, 1, 3):
                pltpu.make_async_remote_copy(
                    src_ref=src.at[layer, half],
                    dst_ref=wbuf.at[slot_here, layer, f, half],
                    send_sem=w_s,
                    recv_sem=w_r.at[slot_here, layer, f],
                    device_id={"section": lax.rem(x + dx, sections), "dp": lax.rem(x, 2)},
                    device_id_type=MESH,
                ).start()
        return 0

    lax.fori_loop(0, layers, send_factors, 0)
    send_raw(2)

    def await_bytes(ref, sem):
        pltpu.make_async_copy(ref, ref, sem).wait()

    def spread_gains(j, layer):
        pick = jnp.where(
            lax.broadcasted_iota(jnp.int32, (16, LANES), 0) == layer, 1.0, 0.0
        ).astype(BF16)
        gains[j, layer] = dot(gpad[j], pick, TN)

    def first_gain(j):
        await_bytes(graw.at[j], n_r.at[j])
        gpad[j, 0 : layers + 1, :] = graw[j]
        spread_gains(j, 0)

    await_bytes(raw_i, raw_r.at[0])
    other_ids = raw_i[...]
    hot[1] = one_hot(other_ids, d, 0.0)
    hot[3] = one_hot(other_ids, d + 2, float(LANES // 2))
    await_bytes(raw_p, raw_r.at[1])
    hbuf[0, 1] = dot(raw_p[...], hot[1], TN)
    hbuf[0, 2] = hbuf[0, 2] + dot(raw_p[...], hot[3], TN)
    first_gain(0)
    first_gain(1)

    def exchange(step, q):
        for i in far_first:
            peer = peer_at(i)
            pltpu.make_async_remote_copy(
                src_ref=st_s.at[step, q],
                dst_ref=st_r.at[step, q, t],
                send_sem=t_s.at[step, q],
                recv_sem=t_r.at[step, q],
                device_id={"tensor": peer},
                device_id_type=MESH,
            ).start()
            pltpu.make_async_remote_copy(
                src_ref=amsg.at[step, q, peer],
                dst_ref=zrecv.at[step, q, t],
                send_sem=m_s.at[step, q],
                recv_sem=m_r.at[step, q],
                device_id={"tensor": peer},
                device_id_type=MESH,
            ).start()
        pltpu.make_async_copy(st_s.at[step, q], st_r.at[step, q, t], t_r.at[step, q]).start()
        pltpu.make_async_copy(amsg.at[step, q, t], zrecv.at[step, q, t], m_r.at[step, q]).start()

    def fwd_send(layer, q):
        j = q // 2

        @pl.when(q != 1)
        def _():
            await_bytes(wbuf.at[j, layer, 0], w_r.at[j, layer, 0])

        h = hbuf[layer, q]
        st_s[layer, q] = jnp.sum(h * h, axis=0, keepdims=True)
        hg[layer, q] = (h * gains[j, layer]).astype(BF16)
        outs = []
        for k in range(blocks):
            out = dot(wbuf[j, layer, 0, k], hg[layer, q, k * bs : (k + 1) * bs, :], TN)
            outs.append(out.reshape(width, 1, rows, LANES))
        message = jnp.concatenate(outs, axis=1).reshape(width, blocks * rows, LANES)
        amsg[layer, q] = message.astype(BF16)
        exchange(layer, q)

    def fold_forward(layer):
        for j in range(2):
            await_bytes(wbuf.at[j, layer, 1], w_r.at[j, layer, 1])
            for m in range(blocks):
                part = slice(m * bs, (m + 1) * bs)
                rp[j, layer, part, :] = dot(wbuf[j, layer, 1, m], perm[part, :], TN).astype(BF16)

    def fold_backward(layer):
        for j in range(2):
            for m in range(blocks):
                part = slice(m * bs, (m + 1) * bs)
                rpt[j, layer, :, part] = dot(perm_t[:, part], wbuf[j, layer, 1, m], NN).astype(BF16)

    def fwd_take(layer, q):
        j = q // 2
        await_bytes(st_r.at[layer, q], t_r.at[layer, q])
        await_bytes(zrecv.at[layer, q], m_r.at[layer, q])
        squares = jnp.sum(st_r[layer, q], axis=0)
        s = lax.rsqrt(squares / model + EPSILON)
        sbuf[layer, q] = s
        arrived = zrecv[layer, q].reshape(feat, LANES)
        for m in range(blocks):
            part = slice(m * bs, (m + 1) * bs)
            b = dot(rp[j, layer, part, :], arrived, NN) * s
            bbuf[layer, q, part, :] = b
            value, steep = gelu_both(b)
            slope[layer, q, part, :] = steep
            hbuf[layer + 1, q, part, :] = hbuf[layer, q, part, :] + value

    def keep_z(layer, q):
        zn[layer, q] = dot(perm[...], zrecv[layer, q].reshape(feat, LANES), NN).astype(BF16)

    def first(q, _):
        fwd_send(0, q)
        return 0

    lax.fori_loop(0, CHUNKS, first, 0)

    def more_gains(layer, _):
        spread_gains(0, layer)
        spread_gains(1, layer)
        return 0

    lax.fori_loop(1, layers + 1, more_gains, 0)
    loads[2].wait()
    await_bytes(raw_t, raw_r.at[2])
    tbuf[0] = dot(own_t[...], hot[0], TN).astype(BF16)
    tbuf[1] = dot(raw_t[...], hot[1], TN).astype(BF16)
    tbuf[2] = (dot(own_t[...], hot[2], TN) + dot(raw_t[...], hot[3], TN)).astype(BF16)

    fold_forward(0)

    def forward(i, _):
        layer = i // CHUNKS
        q = lax.rem(i, CHUNKS)
        fwd_take(layer, q)
        fwd_send(layer + 1, q)
        keep_z(layer, q)

        @pl.when(q == CHUNKS - 1)
        def _():
            fold_forward(layer + 1)

        return 0

    lax.fori_loop(0, CHUNKS * (layers - 1), forward, 0)

    def last(q, _):
        fwd_take(layers - 1, q)
        j = q // 2
        h = hbuf[layers, q]
        gh = gains[j, layers] * h
        fst_s[q, 0] = jnp.sum(h * h, axis=0, keepdims=True)
        fst_s[q, 1] = jnp.sum(gh * gh, axis=0, keepdims=True)
        fst_s[q, 2] = jnp.sum(gh * tbuf[q].astype(F32), axis=0, keepdims=True)

        for i in far_first:
            pltpu.make_async_remote_copy(
                src_ref=fst_s.at[q],
                dst_ref=fst_r.at[q, t],
                send_sem=f_s.at[q],
                recv_sem=f_r.at[q],
                device_id={"tensor": peer_at(i)},
                device_id_type=MESH,
            ).start()
        pltpu.make_async_copy(fst_s.at[q], fst_r.at[q, t], f_r.at[q]).start()
        keep_z(layers - 1, q)
        return 0

    lax.fori_loop(0, CHUNKS, last, 0)
    fold_backward(layers - 1)
    fold_backward(layers - 2)

    def send_grad(layer, f, j):
        critic = d + 2 * j
        for e in range(2):
            piece = gsend.at[j, layer, f, pl.ds(2 * e, 2)]
            landing = grecv.at[layer, f, x]
            stays = (critic == x) & (d == e)

            @pl.when(stays)
            def _():
                pltpu.make_async_copy(piece, landing, g_r.at[layer, f]).start()

            @pl.when(jnp.logical_not(stays))
            def _():
                pltpu.make_async_remote_copy(
                    src_ref=piece,
                    dst_ref=landing,
                    send_sem=g_s.at[j, layer, f],
                    recv_sem=g_r.at[layer, f],
                    device_id={"section": critic, "dp": e},
                    device_id_type=MESH,
                ).start()

    def factor_grad(layer, f, q, lhs, rhs):
        @pl.when(q == 1)
        def _():
            for k in range(blocks):
                part = slice(k * bs, (k + 1) * bs)
                acts = jnp.concatenate((lhs[layer, 0, part, :], lhs[layer, 1, part, :]), axis=1)
                backs = jnp.concatenate((rhs[0, part, :], rhs[1, part, :]), axis=1)
                gsend[0, layer, f, k] = dot(acts, backs, NT).astype(BF16)
            send_grad(layer, f, 0)

        @pl.when(q == 2)
        def _():
            for k in range(blocks):
                part = slice(k * bs, (k + 1) * bs)
                gsend[1, layer, f, k] = dot(lhs[layer, 2, part, :], rhs[2, part, :], NT).astype(BF16)
            send_grad(layer, f, 1)

    def bwd_send(layer, q):
        j = q // 2
        step = layers + layer
        gbs = gbuf[q] * slope[layer, q] * sbuf[layer, q]
        st_s[step, q] = jnp.sum(gbs * bbuf[layer, q], axis=0, keepdims=True)
        gb16[q] = gbs.astype(BF16)
        moved = dot(rpt[j, layer], gb16[q], NN)
        amsg[step, q] = moved.astype(BF16).reshape(width, blocks * rows, LANES)
        exchange(step, q)

    def bwd_land(layer, q):
        step = layers + layer
        await_bytes(st_r.at[step, q], t_r.at[step, q])
        await_bytes(zrecv.at[step, q], m_r.at[step, q])
        arrived = zrecv[step, q].astype(F32).reshape(width, blocks, rows, LANES)
        for k in range(blocks):
            part = slice(k * bs, (k + 1) * bs)
            ga16[q, part, :] = arrived[:, k].reshape(bs, LANES).astype(BF16)

    def bwd_norm(layer, q):
        j = q // 2
        inner = jnp.sum(st_r[layers + layer, q], axis=0)
        coefficient = sbuf[layer, q] * inner / model
        for k in range(blocks):
            part = slice(k * bs, (k + 1) * bs)
            gu = dot(wbuf[j, layer, 0, k], ga16[q, part, :], NN)
            gbuf[q, part, :] = (
                gbuf[q, part, :]
                + gu * gains[j, layer, part, :]
                - hbuf[layer, q, part, :] * coefficient
            )

    grad_factor = 1.0 / math.sqrt(2 * total_tokens)
    outs = (gl_out, gr_out)

    def finish(layer):
        for f in (1, 0):
            await_bytes(grecv.at[layer, f], g_r.at[layer, f])
            total = grecv[layer, f, 0].astype(F32)
            for source in range(1, sections):
                total = total + grecv[layer, f, source].astype(F32)
            fin[layer, f] = total * grad_factor
            pltpu.make_async_remote_copy(
                src_ref=fin.at[layer, f],
                dst_ref=outs[f].at[layer, half],
                send_sem=o_s,
                recv_sem=o_r,
                device_id=partner,
                device_id_type=MESH,
            ).start()
            pltpu.make_async_copy(fin.at[layer, f], outs[f].at[layer, half], o_l).start()

    def turn(q, _):
        j = q // 2
        await_bytes(fst_r.at[q], f_r.at[q])
        sums = jnp.sum(fst_r[q], axis=0)
        s = lax.rsqrt(sums[0] / model + EPSILON)
        coefficient = s * s * s * (s * sums[1] - sums[2]) / model
        h = hbuf[layers, q]
        gain = gains[j, layers]
        e = (h * s * gain - tbuf[q].astype(F32)) * gain
        gbuf[q] = s * e - h * coefficient
        bwd_send(layers - 1, q)
        factor_grad(layers - 1, 1, q, zn, gb16)
        return 0

    lax.fori_loop(0, CHUNKS, turn, 0)

    def backward(i, _):
        layer = layers - 1 - i // CHUNKS
        q = lax.rem(i, CHUNKS)
        bwd_land(layer, q)
        bwd_norm(layer, q)
        bwd_send(layer - 1, q)
        factor_grad(layer, 0, q, hg, ga16)
        factor_grad(layer - 1, 1, q, zn, gb16)

        @pl.when((q == CHUNKS - 1) & (layer == 1))
        def _():
            finish(3)

        @pl.when((q == CHUNKS - 1) & (layer > 1))
        def _():
            fold_backward(layer - 2)

        return 0

    lax.fori_loop(0, CHUNKS * (layers - 1), backward, 0)

    def ending(q, _):
        bwd_land(0, q)
        factor_grad(0, 0, q, hg, ga16)
        bwd_norm(0, q)

        @pl.when(q == 1)
        def _():
            finish(2)

        return 0

    lax.fori_loop(0, CHUNKS, ending, 0)

    lead_own = gbuf[0].astype(BF16)
    lead_other = gbuf[1].astype(BF16)
    trail = gbuf[2].astype(BF16)
    d_s[...] = (dot(hot[1], lead_other, NT) + dot(hot[3], trail, NT)).astype(BF16)
    back = pltpu.make_async_remote_copy(
        src_ref=d_s,
        dst_ref=d_r,
        send_sem=e_s,
        recv_sem=e_r,
        device_id=partner,
        device_id_type=MESH,
    )
    back.start()
    own = dot(hot[0], lead_own, NT) + dot(hot[2], trail, NT)
    finish(1)

    def drain(step, _):
        def one(q, _):
            await_bytes(amsg.at[step, q, pl.ds(0, width - 1)], m_s.at[step, q])
            await_bytes(st_r.at[step, q, pl.ds(0, width - 1)], t_s.at[step, q])
            return 0

        return lax.fori_loop(0, CHUNKS, one, 0)

    lax.fori_loop(0, 2 * layers, drain, 0)

    def drain_final(q, _):
        await_bytes(fst_r.at[q, pl.ds(0, width - 1)], f_s.at[q])
        return 0

    lax.fori_loop(0, CHUNKS, drain_final, 0)
    for at, (src, dst) in enumerate(raws):
        await_bytes(dst, raw_s.at[at])
    await_bytes(wbuf.at[:, pl.ds(0, 3)], w_s)
    for at in range(sections - 1):
        await_bytes(graw.at[0, :, pl.ds(0, feat // 2)], n_s.at[at])

    back.wait()
    d_out[...] = ((own + d_r[...].astype(F32)) * 0.5).astype(BF16)
    finish(0)

    def drain_grad(layer, _):
        for j in range(2):
            for f in range(2):
                local = (d + 2 * j) == x

                @pl.when(local)
                def _():
                    await_bytes(gsend.at[j, layer, f, pl.ds(0, 2)], g_s.at[j, layer, f])

                @pl.when(jnp.logical_not(local))
                def _():
                    await_bytes(gsend.at[j, layer, f], g_s.at[j, layer, f])

        return 0

    lax.fori_loop(0, layers, drain_grad, 0)
    await_bytes(fin, o_l)
    await_bytes(fin, o_s)
    await_bytes(fin, o_r)


def publish_kernel(d_in, gl_in, gr_in, d_out, gl_out, gr_out, sems):
    layers = gl_in.shape[0]
    moves = [(d_in, d_out)]
    for src, dst in ((gl_in, gl_out), (gr_in, gr_out)):
        for layer in range(layers):
            moves.append((src.at[layer], dst.at[layer]))
    copies = [
        pltpu.make_async_copy(src, dst, sems.at[at]) for at, (src, dst) in enumerate(moves)
    ]
    for copy in copies:
        copy.start()
    for copy in copies:
        copy.wait()


def publish(*arrays):
    anyspace = pl.BlockSpec(memory_space=pl.ANY)
    return pl.pallas_call(
        publish_kernel,
        out_shape=tuple(jax.ShapeDtypeStruct(a.shape, a.dtype) for a in arrays),
        in_specs=[anyspace] * 3,
        out_specs=(pl.BlockSpec(memory_space=pltpu.HBM),) * 3,
        scratch_shapes=[pltpu.SemaphoreType.DMA((1 + 2 * arrays[1].shape[0],))],
        compiler_params=pltpu.CompilerParams(vmem_limit_bytes=16 * 1024 * 1024),
        name="publish",
    )(*arrays)


def shards(width, patches, teacher, critic_pairs, left_factors, right_factors, norm_gains):
    tok, feat = patches.shape
    layers, blocks, bs = left_factors.shape[1:4]
    rows = bs // width
    steps = 2 * layers
    total_tokens = tok * 8
    vmem = pl.BlockSpec(memory_space=pltpu.VMEM)
    anyspace = pl.BlockSpec(memory_space=pl.ANY)
    tile = (feat, LANES)
    message = (steps, CHUNKS, width, blocks * rows, LANES)
    dma = pltpu.SemaphoreType.DMA
    scratch = [
        pltpu.VMEM((tok, feat), BF16),
        pltpu.VMEM((tok, feat), BF16),
        pltpu.VMEM((2, tok), jnp.int32),
        pltpu.VMEM((tok, feat), BF16),
        pltpu.VMEM((tok, feat), BF16),
        pltpu.VMEM((2, tok), jnp.int32),
        pltpu.VMEM((2, layers, 2, blocks, bs, bs), BF16),
        pltpu.VMEM((2, layers + 1, feat), BF16),
        pltpu.VMEM((2, 16, feat), BF16),
        pltpu.VMEM((2, layers + 1) + tile, F32),
        pltpu.VMEM((feat, feat), BF16),
        pltpu.VMEM((feat, feat), BF16),
        pltpu.VMEM((2, layers, feat, feat), BF16),
        pltpu.VMEM((2, layers, feat, feat), BF16),
        pltpu.VMEM((4, tok, LANES), BF16),
        pltpu.VMEM((layers + 1, CHUNKS) + tile, F32),
        pltpu.VMEM((layers, CHUNKS) + tile, BF16),
        pltpu.VMEM((layers, CHUNKS) + tile, BF16),
        pltpu.VMEM((layers, CHUNKS) + tile, F32),
        pltpu.VMEM((layers, CHUNKS) + tile, F32),
        pltpu.VMEM((layers, CHUNKS, 1, LANES), F32),
        pltpu.VMEM((CHUNKS,) + tile, F32),
        pltpu.VMEM((CHUNKS,) + tile, BF16),
        pltpu.VMEM((CHUNKS,) + tile, BF16),
        pltpu.VMEM((CHUNKS,) + tile, BF16),
        pltpu.VMEM(message, BF16),
        pltpu.VMEM(message, BF16),
        pltpu.VMEM((steps, CHUNKS, 1, LANES), F32),
        pltpu.VMEM((steps, CHUNKS, width, 1, LANES), F32),
        pltpu.VMEM((CHUNKS, 3, 1, LANES), F32),
        pltpu.VMEM((CHUNKS, width, 3, 1, LANES), F32),
        pltpu.VMEM((2, layers, 2, blocks, bs, bs), BF16),
        pltpu.VMEM((layers, 2, 4, 2, bs, bs), BF16),
        pltpu.VMEM((layers, 2, 2, bs, bs), F32),
        pltpu.VMEM((tok, feat), BF16),
        pltpu.VMEM((tok, feat), BF16),
        dma((steps, CHUNKS)),
        dma((steps, CHUNKS)),
        dma((steps, CHUNKS)),
        dma((steps, CHUNKS)),
        dma((CHUNKS,)),
        dma((CHUNKS,)),
        dma,
        dma((2, layers, 2)),
        dma((3,)),
        dma((2,)),
        dma((3,)),
        dma((3,)),
        dma((2, layers, 2)),
        dma((layers, 2)),
        dma,
        dma,
        dma,
        dma,
        dma,
        dma((3,)),
    ]
    operands = (
        patches,
        teacher,
        critic_pairs.T,
        left_factors[0],
        right_factors[0],
        norm_gains[0],
    )
    grad_shape = jax.ShapeDtypeStruct((layers, blocks, bs, bs), F32)
    d_patches, grad_left, grad_right = pl.pallas_call(
        functools.partial(kernel, width, layers, blocks, total_tokens),
        out_shape=(jax.ShapeDtypeStruct((tok, feat), BF16), grad_shape, grad_shape),
        in_specs=[anyspace] * 6,
        out_specs=(vmem, anyspace, anyspace),
        scratch_shapes=scratch,
        compiler_params=pltpu.CompilerParams(
            collective_id=0, has_side_effects=True, vmem_limit_bytes=48 * 1024 * 1024
        ),
        name="critics",
    )(*(pltpu.with_memory_space_constraint(a, pltpu.HBM) for a in operands))
    d_patches, grad_left, grad_right = publish(d_patches, grad_left, grad_right)
    return d_patches, grad_left[None], grad_right[None]


def solution(mesh):
    in_specs = (
        P(("section", "dp"), "tensor"),
        P(("section", "dp"), "tensor"),
        P(("section", "dp"), None),
        P("section", None, "tensor", None, None),
        P("section", None, "tensor", None, None),
        P("section", None, "tensor"),
    )
    out_specs = (
        P(("section", "dp"), "tensor"),
        P("section", None, "tensor", None, None),
        P("section", None, "tensor", None, None),
    )
    body = functools.partial(shards, mesh.shape["tensor"])
    return jax.shard_map(body, mesh=mesh, in_specs=in_specs, out_specs=out_specs, check_vma=False)
```
